512 devices in a mesh: tok: 32 (over y_hi, z, core), head: 16 (over y_lo, x).
Axes of the slice: x: 4, y: 8 (y_hi: 2, y_lo: 4; y = y_hi * 4 + y_lo), z: 8, core: 2. Of those that a mesh axis runs over, the one named last changes fastest.
Arguments:
- queries: bfloat16 [4096, 4096], P('tok', 'head'), may hold values from -512 to 512
- kv: bfloat16 [4, 4096, 128], P(None, 'tok', 'head'), may hold values from -6 to 6
- w_out: bfloat16 [4096, 8192], P('head', 'tok'), may hold values from -0.09375 to 0.09375
Outputs:
- projected: bfloat16 [4096, 8192], P('head', 'tok')
The draws below stay inside these ranges and needn't reach their ends.
All inputs are finite; a program needn't handle non-finite values.
Results may differ from the reference program's by a relative error of at most 0.011.
Values may be sent and summed in bfloat16 or wider, within the bound.
No kernel may reach another device: no remote copies, remote signals or barrier semaphores. Data moves between devices by JAX's collectives and lax.ppermute only.
A program may use at most 64 MiB of HBM per device.

```python
import math
import jax
import jax.numpy as jnp
from jax import lax

D = 8192
HQ = 32
HD = 128
W1 = 512
W2 = 32
TOKENS = 4096


def shared_fields(key):
    base_key = jax.random.fold_in(key, 7)
    key_fields, key_queries = jax.random.split(base_key)
    fields = jnp.clip(jax.random.normal(key_fields, (4, TOKENS, HD), jnp.float32), -6.0, 6.0)
    queries = jnp.clip(jax.random.normal(key_queries, (TOKENS, HQ * HD), jnp.float32), -6.0, 6.0)
    return (fields, queries)


def draw_kv(key, part):
    return shared_fields(key)[0].astype(jnp.bfloat16)


def draw_queries(key, part):
    return shared_fields(key)[1].astype(jnp.bfloat16)


def block_levels(stream_key, extent, cuts, smallest, largest):
    factor_of, own = 1.0, jax.random.fold_in(stream_key, 6)
    for axis_at, blocks in cuts:
        heights = jnp.exp(jax.random.uniform(jax.random.fold_in(own, axis_at), (blocks,), jnp.float32, smallest / len(cuts), largest / len(cuts)))
        factor_of = factor_of * jnp.repeat(heights, extent[axis_at] // blocks).reshape([-1 if axis == axis_at else 1 for axis in range(len(extent))])
    return factor_of


def gaussian(rng, dims, deviation, bound, cuts=(), kind=jnp.bfloat16):
    factor_of = block_levels(rng, dims, cuts, -0.22, 0.18) if cuts else 1.0
    values = jax.random.normal(rng, dims, jnp.float32) * deviation * factor_of
    return jnp.minimum(jnp.maximum(values, -bound), bound).astype(kind)


def setup_inputs(seed: int = 0) -> dict:
    splits = jax.random.split(jax.random.key(seed), 4)
    queries = draw_queries(jax.random.fold_in(splits[3], 71), 0)
    kv = draw_kv(jax.random.fold_in(splits[3], 71), 0)
    w_out = gaussian(splits[2], (HQ * HD, D), (HQ * HD) ** -0.5, 0.09375, ((0, 16), (1, 32)))
    return {"queries": queries, "kv": kv, "w_out": w_out}


def window_masks(first_anchor, second_anchor):
    query_pos = jnp.arange(8)[:, None]
    first_slot = jnp.arange(W1 + 8)[None, :]
    second_slot = jnp.arange(W2 + 8)[None, :]
    allowed_first = (first_slot > query_pos) & (first_slot <= query_pos + W1) & (first_anchor + first_slot >= 0)
    allowed_second = (second_slot > query_pos) & (second_slot <= query_pos + W2) & (second_anchor + second_slot >= 0)
    return (allowed_first, allowed_second)

def attend(query_part, first_keys, second_keys, allowed_first, allowed_second):
    score_scale = 3.0 / math.sqrt(query_part.shape[-1])
    query_key = (query_part.astype(jnp.float32)[:, :, None, :] * second_keys[0].astype(jnp.float32)[None, None, :, :]).astype(jnp.bfloat16)
    pair_shape = query_key.shape[:3]
    flattened = query_key.reshape(-1, query_key.shape[-1])
    scores = jnp.dot(flattened, first_keys[0].T, preferred_element_type=jnp.float32)
    scores = scores.reshape(pair_shape + (first_keys.shape[1],)) * score_scale
    allowed = allowed_second[:, None, :, None] & allowed_first[:, None, None, :]
    scores = jnp.where(allowed, scores, -jnp.inf)
    row_max = lax.optimization_barrier(jnp.max(scores, axis=(2, 3), keepdims=True))
    exponent = jnp.exp(scores - row_max)
    denominator = lax.optimization_barrier(jnp.sum(exponent, axis=(2, 3)))
    weights = exponent.astype(jnp.bfloat16)
    value_mix = jnp.dot(weights.reshape(-1, first_keys.shape[1]), first_keys[1], preferred_element_type=jnp.float32)
    value_mix = value_mix.reshape(pair_shape + (first_keys.shape[2],))
    attended = lax.optimization_barrier(jnp.sum(value_mix * second_keys[1].astype(jnp.float32)[None, None, :, :], axis=2))
    return (attended / denominator[:, :, None]).astype(jnp.bfloat16)

def reference(queries, kv, w_out):
    head_count = queries.shape[1] // HD
    padded = jnp.pad(kv, ((0, 0), (W1, 0), (0, 0)))

    def block(block_index):
        offset = block_index * 8
        query_part = lax.dynamic_slice_in_dim(queries, offset, 8, 0).reshape(8, head_count, HD)
        first_part = lax.dynamic_slice_in_dim(padded[0:2], offset, W1 + 8, 1)
        second_part = lax.dynamic_slice_in_dim(padded[2:4], offset + W1 - W2, W2 + 8, 1)
        allowed_first, allowed_second = window_masks(offset - W1, offset - W2)
        return attend(query_part, first_part, second_part, allowed_first, allowed_second).reshape(8, head_count * HD)
    attention = lax.map(block, jnp.arange(TOKENS // 8).astype(jnp.int32)).reshape(TOKENS, head_count * HD)
    return jnp.dot(attention, w_out, preferred_element_type=jnp.float32).astype(jnp.bfloat16)
```

```python
import functools
import math

import jax
import jax.numpy as jnp
from jax import lax
from jax.experimental import pallas as pl
from jax.experimental.pallas import tpu as pltpu
from jax.sharding import Mesh, PartitionSpec as P

HD = 128
W1 = 512
W2 = 32
BLOCK = 128
STEP = 8
TOK = ("yh", "z", "core")
HEAD = ("yl", "x")
ALL = TOK + HEAD
SIZES = (2, 8, 2, 4, 4)
FAR = -1e30
BF16 = jnp.bfloat16
F32 = jnp.float32


def flat(yh, z, core, yl, x):
    return (((yh * 8 + z) * 2 + core) * 4 + yl) * 4 + x


def places():
    for yh in range(2):
        for z in range(8):
            for core in range(2):
                for yl in range(4):
                    for x in range(4):
                        yield yh, z, core, yl, x


def attention_pairs():
    return [
        (flat(yh, z, core, yl, x), flat(yl // 2, 2 * x + core, yl % 2, 2 * yh + z // 4, z % 4))
        for yh, z, core, yl, x in places()
    ]


def weight_pairs():
    return [
        (flat(yh, z, core, yl, x), flat(yl // 2, z, yl % 2, 2 * yh + core, x))
        for yh, z, core, yl, x in places()
    ]


def attend_kernel(where_ref, q_ref, kv_ref, out_ref, k1_ref, v1_ref, k2_ref, v2_ref, live_ref, q32_ref, acc_ref):
    block = where_ref[0]
    scale = 3.0 / math.sqrt(HD) * math.log2(math.e)

    def piece(k):
        return kv_ref[:, 8 * k : 8 * k + 8, :].astype(F32).reshape(HD, BLOCK)

    for k in range(5):
        k1_ref[:, BLOCK * k : BLOCK * (k + 1)] = piece(k).astype(BF16)
        v1_ref[BLOCK * k : BLOCK * (k + 1), 0:HD] = piece(5 + k).T.astype(BF16)
    v1_ref[:, HD : 2 * HD] = jnp.ones((5 * BLOCK, HD), BF16)
    first = block == 0
    own_k2 = piece(11).T
    k2_ref[W2:, :] = own_k2
    k2_ref[0:W2, :] = jnp.where(first, jnp.broadcast_to(own_k2[0:1, :], (W2, HD)), piece(10).T[BLOCK - W2 :, :])
    v2_ref[W2:, :] = piece(13).T
    v2_ref[0:W2, :] = jnp.where(first, 0.0, piece(12).T[BLOCK - W2 :, :])
    live_ref[W2:, :] = jnp.ones((BLOCK, HD), F32)
    live_ref[0:W2, :] = jnp.where(first, jnp.zeros((W2, HD), F32), 1.0)
    q32_ref[...] = q_ref[...].astype(F32)
    bias = [jnp.where(block - 4 + k < 0, FAR, 0.0) for k in range(4)]
    column = lax.broadcasted_iota(jnp.int32, (STEP, BLOCK), 1)
    row = lax.broadcasted_iota(jnp.int32, (STEP, BLOCK), 0)

    def step(index, carry):
        start = pl.multiple_of(index * STEP, STEP)
        newer = column > row + start
        newer_all = jnp.broadcast_to(newer[None], (W2, STEP, BLOCK)).reshape(W2 * STEP, BLOCK)
        tile_bias = [jnp.where(newer, bias[0], 0.0)] + [jnp.full((STEP, BLOCK), bias[k], F32) for k in (1, 2, 3)]
        for head in range(2):
            query = q32_ref[pl.ds(start, STEP), HD * head : HD * (head + 1)]
            rows = [query * k2_ref[pl.ds(start + W2 - back, STEP), :] for back in range(W2)]
            query_key = jnp.concatenate(rows, axis=0).astype(BF16)
            scores = jnp.dot(query_key, k1_ref[...], preferred_element_type=F32)
            tiles = [jnp.where(newer_all, scores[:, 0:BLOCK], scores[:, 4 * BLOCK :])]
            tiles += [scores[:, BLOCK * k : BLOCK * (k + 1)] for k in (1, 2, 3)]
            peak = None
            for k in range(4):
                top = jnp.max(tiles[k].reshape(W2, STEP, BLOCK), axis=0) + tile_bias[k]
                peak = top if peak is None else jnp.maximum(peak, top)
            peak = jnp.max(peak, axis=1, keepdims=True) * scale
            weights = []
            for k in range(4):
                offset = tile_bias[k] - peak
                grown = tiles[k].reshape(W2, STEP, BLOCK) * scale + offset[None]
                weights.append(jnp.exp2(grown).reshape(W2 * STEP, BLOCK))
            mixed = [jnp.where(newer_all, weights[0], 0.0)] + weights[1:] + [jnp.where(newer_all, 0.0, weights[0])]
            mixed = jnp.concatenate([m.astype(BF16) for m in mixed], axis=1)
            value = jnp.dot(mixed, v1_ref[...], preferred_element_type=F32)
            total = jnp.zeros((STEP, HD), F32)
            denominator = jnp.zeros((STEP, HD), F32)
            for back in range(W2):
                part = value[STEP * back : STEP * (back + 1), :]
                total += part[:, 0:HD] * v2_ref[pl.ds(start + W2 - back, STEP), :]
                denominator += part[:, HD:] * live_ref[pl.ds(start + W2 - back, STEP), :]
            acc_ref[pl.ds(start, STEP), HD * head : HD * (head + 1)] = total / denominator
        return carry

    lax.fori_loop(0, BLOCK // STEP, step, 0)
    out_ref[...] = acc_ref[...].astype(BF16)


def attend(block, queries, window):
    return pl.pallas_call(
        attend_kernel,
        out_shape=jax.ShapeDtypeStruct((BLOCK, 2 * HD), BF16),
        in_specs=[
            pl.BlockSpec(memory_space=pltpu.SMEM),
            pl.BlockSpec(memory_space=pltpu.VMEM),
            pl.BlockSpec(memory_space=pltpu.VMEM),
        ],
        out_specs=pl.BlockSpec(memory_space=pltpu.VMEM),
        scratch_shapes=[
            pltpu.VMEM((HD, 5 * BLOCK), BF16),
            pltpu.VMEM((5 * BLOCK, 2 * HD), BF16),
            pltpu.VMEM((W2 + BLOCK, HD), F32),
            pltpu.VMEM((W2 + BLOCK, HD), F32),
            pltpu.VMEM((W2 + BLOCK, HD), F32),
            pltpu.VMEM((BLOCK, 2 * HD), F32),
            pltpu.VMEM((BLOCK, 2 * HD), F32),
        ],
        cost_estimate=pl.CostEstimate(flops=6_000_000_000, bytes_accessed=1_000_000, transcendentals=4_200_000),
        name="attend",
    )(block, queries, window)


def project_kernel(core_ref, a_ref, w_ref, keep_ref, send_ref):
    core = core_ref[0]
    for half in range(2):
        for slot in range(2):
            block = 2 * half + (core if slot == 0 else 1 - core)
            total = jnp.zeros((256, 256), F32)
            for x in range(4):
                total += jnp.dot(a_ref[x], w_ref[block, x], preferred_element_type=F32)
            if slot == 0:
                keep_ref[half] = total
            else:
                send_ref[half] = total.astype(send_ref.dtype)


def project(core, attention, weights):
    return pl.pallas_call(
        project_kernel,
        out_shape=(jax.ShapeDtypeStruct((2, 256, 256), F32), jax.ShapeDtypeStruct((2, 256, 256), F32)),
        in_specs=[
            pl.BlockSpec(memory_space=pltpu.SMEM),
            pl.BlockSpec(memory_space=pltpu.VMEM),
            pl.BlockSpec(memory_space=pltpu.VMEM),
        ],
        out_specs=(pl.BlockSpec(memory_space=pltpu.VMEM), pl.BlockSpec(memory_space=pltpu.VMEM)),
        cost_estimate=pl.CostEstimate(flops=540_000_000, bytes_accessed=4_000_000, transcendentals=0),
        name="project",
    )(core, attention, weights)


def chip_shift(x, by):
    pairs = []
    for chip in range(16 - by):
        other = chip + by
        for core in range(2):
            pairs.append((2 * chip + core, 2 * other + core))
    return lax.ppermute(x, TOK, pairs)


def body(queries, kv, w_out):
    yh = lax.axis_index("yh")
    core = lax.axis_index("core")
    block = lax.axis_index(TOK).astype(jnp.int32)
    raw = jnp.transpose(kv, (0, 2, 1))
    swap = [(0, 1), (1, 0)]
    with jax.named_scope("kv_core"):
        other = lax.ppermute(raw, "core", swap)
    pair = jnp.where(core == 0, jnp.stack([raw, other]), jnp.stack([other, raw]))
    with jax.named_scope("kv_chip1"):
        near = chip_shift(pair, 1)
    with jax.named_scope("kv_chip2"):
        far = chip_shift(pair[:, 0:2], 2)
    firsts = jnp.concatenate([far, near[:, 0:2], pair[:, 0:2]], axis=0)
    seconds = jnp.concatenate([near[1:2, 2:4], pair[:, 2:4]], axis=0)
    firsts = lax.dynamic_slice_in_dim(firsts, core, 5, 0)
    seconds = lax.dynamic_slice_in_dim(seconds, core, 2, 0)
    window = jnp.concatenate(
        [firsts[:, 0].reshape(40, 128), firsts[:, 1].reshape(40, 128), seconds[:, 0].reshape(16, 128), seconds[:, 1].reshape(16, 128)],
        axis=0,
    )
    with jax.named_scope("kv_head"):
        window = lax.all_to_all(jnp.broadcast_to(window[None], (16,) + window.shape), HEAD, 0, 0)
    with jax.named_scope("w_move"):
        moved = lax.ppermute(w_out, ALL, weight_pairs())
    with jax.named_scope("w_head"):
        weights = lax.all_to_all(jnp.broadcast_to(moved[None], (16,) + moved.shape), HEAD, 0, 0)
    weights = weights.reshape(4, 4, 256, 256)
    attention = attend(block.reshape(1), queries, window)
    with jax.named_scope("att_move"):
        attention = lax.ppermute(attention, ALL, attention_pairs())
    with jax.named_scope("att_z"):
        attention = lax.all_to_all(jnp.broadcast_to(attention[None], (8,) + attention.shape), "z", 0, 0)
    keep, send = project(core.astype(jnp.int32).reshape(1), attention.reshape(4, 256, 256), weights)
    with jax.named_scope("out_core"):
        got = lax.ppermute(send, "core", swap)
    summed = keep + got
    leaving = lax.dynamic_index_in_dim(summed, 1 - yh, 0, keepdims=False).astype(BF16)
    with jax.named_scope("out_yh"):
        arrived = lax.ppermute(leaving, "yh", swap)
    staying = lax.dynamic_index_in_dim(summed, yh, 0, keepdims=False)
    return (staying + arrived.astype(F32)).astype(BF16)


def solution(mesh):
    fine = Mesh(mesh.devices.reshape(SIZES), ALL)
    return jax.shard_map(
        body,
        mesh=fine,
        in_specs=(P(TOK, HEAD), P(None, TOK, HEAD), P(HEAD, TOK)),
        out_specs=P(HEAD, TOK),
        check_vma=False,
    )
```

```python
import math

import jax
import jax.numpy as jnp
from jax import lax
from jax.experimental import pallas as pl
from jax.experimental.pallas import tpu as pltpu
from jax.sharding import Mesh, PartitionSpec as P


HD = 128
W2 = 32
BLOCK = 128
STEP = 8
TOK = ("yh", "z", "core")
HEAD = ("yl", "x")
ALL = TOK + HEAD
SIZES = (2, 8, 2, 4, 4)
FAR = -1e30
BF16 = jnp.bfloat16
F32 = jnp.float32


def flat(yh, z, core, yl, x):
    return (((yh * 8 + z) * 2 + core) * 4 + yl) * 4 + x


def places():
    for yh in range(2):
        for z in range(8):
            for core in range(2):
                for yl in range(4):
                    for x in range(4):
                        yield yh, z, core, yl, x


def attention_pairs():
    return [
        (flat(yh, z, core, yl, x), flat(yl // 2, 2 * x + core, yl % 2, 2 * yh + z // 4, z % 4))
        for yh, z, core, yl, x in places()
    ]


def weight_pairs():
    return [
        (flat(yh, z, core, yl, x), flat(yl // 2, z, yl % 2, 2 * yh + core, x))
        for yh, z, core, yl, x in places()
    ]


def attend_kernel(where_ref, q_ref, kv_ref, out_ref, k1_ref, v1_ref, k2_ref, v2_ref, live_ref, q32_ref, acc_ref):
    block = where_ref[0]
    scale = 3.0 / math.sqrt(HD) * math.log2(math.e)

    def piece(k):
        return kv_ref[:, 8 * k : 8 * k + 8, :].astype(F32).reshape(HD, BLOCK)

    for k in range(5):
        k1_ref[:, BLOCK * k : BLOCK * (k + 1)] = piece(k).astype(BF16)
        v1_ref[BLOCK * k : BLOCK * (k + 1), 0:HD] = piece(5 + k).T.astype(BF16)
    v1_ref[:, HD : 2 * HD] = jnp.ones((5 * BLOCK, HD), BF16)
    first = block == 0
    own_k2 = piece(11).T
    k2_ref[W2:, :] = own_k2
    k2_ref[0:W2, :] = jnp.where(first, jnp.broadcast_to(own_k2[0:1, :], (W2, HD)), piece(10).T[BLOCK - W2 :, :])
    v2_ref[W2:, :] = piece(13).T
    v2_ref[0:W2, :] = jnp.where(first, 0.0, piece(12).T[BLOCK - W2 :, :])
    live_ref[W2:, :] = jnp.ones((BLOCK, HD), F32)
    live_ref[0:W2, :] = jnp.where(first, jnp.zeros((W2, HD), F32), 1.0)
    q32_ref[...] = q_ref[...].astype(F32)
    bias = [jnp.where(block - 4 + k < 0, FAR, 0.0) for k in range(4)]
    column = lax.broadcasted_iota(jnp.int32, (STEP, BLOCK), 1)
    row = lax.broadcasted_iota(jnp.int32, (STEP, BLOCK), 0)

    def step(index, carry):
        start = pl.multiple_of(index * STEP, STEP)
        newer = column > row + start
        newer_all = jnp.broadcast_to(newer[None], (W2, STEP, BLOCK)).reshape(W2 * STEP, BLOCK)
        tile_bias = [jnp.where(newer, bias[0], 0.0)] + [jnp.full((STEP, BLOCK), bias[k], F32) for k in (1, 2, 3)]
        for head in range(2):
            query = q32_ref[pl.ds(start, STEP), HD * head : HD * (head + 1)]
            rows = [query * k2_ref[pl.ds(start + W2 - back, STEP), :] for back in range(W2)]
            query_key = jnp.concatenate(rows, axis=0).astype(BF16)
            scores = jnp.dot(query_key, k1_ref[...], preferred_element_type=F32)
            tiles = [jnp.where(newer_all, scores[:, 0:BLOCK], scores[:, 4 * BLOCK :])]
            tiles += [scores[:, BLOCK * k : BLOCK * (k + 1)] for k in (1, 2, 3)]
            peak = None
            for k in range(4):
                top = jnp.max(tiles[k].reshape(W2, STEP, BLOCK), axis=0) + tile_bias[k]
                peak = top if peak is None else jnp.maximum(peak, top)
            peak = jnp.max(peak, axis=1, keepdims=True) * scale
            weights = []
            for k in range(4):
                offset = tile_bias[k] - peak
                grown = tiles[k].reshape(W2, STEP, BLOCK) * scale + offset[None]
                weights.append(jnp.exp2(grown).reshape(W2 * STEP, BLOCK))
            mixed = [jnp.where(newer_all, weights[0], 0.0)] + weights[1:] + [jnp.where(newer_all, 0.0, weights[0])]
            mixed = jnp.concatenate([m.astype(BF16) for m in mixed], axis=1)
            value = jnp.dot(mixed, v1_ref[...], preferred_element_type=F32)
            total = jnp.zeros((STEP, HD), F32)
            denominator = jnp.zeros((STEP, HD), F32)
            for back in range(W2):
                part = value[STEP * back : STEP * (back + 1), :]
                total += part[:, 0:HD] * v2_ref[pl.ds(start + W2 - back, STEP), :]
                denominator += part[:, HD:] * live_ref[pl.ds(start + W2 - back, STEP), :]
            acc_ref[pl.ds(start, STEP), HD * head : HD * (head + 1)] = total / denominator
        return carry

    lax.fori_loop(0, BLOCK // STEP, step, 0)
    out_ref[...] = acc_ref[...].astype(BF16)


def window_kernel(parity_ref, all_ref, out_ref):
    parity = parity_ref[0]
    for column in range(16):
        last = 2 * column + parity
        for k in range(5):
            source = jnp.maximum(last - 4 + k, 0)
            out_ref[column, 8 * k : 8 * (k + 1), :] = all_ref[source, 0]
            out_ref[column, 8 * (5 + k) : 8 * (6 + k), :] = all_ref[source, 1]
        for k in range(2):
            source = jnp.maximum(last - 1 + k, 0)
            out_ref[column, 8 * (10 + k) : 8 * (11 + k), :] = all_ref[source, 2]
            out_ref[column, 8 * (12 + k) : 8 * (13 + k), :] = all_ref[source, 3]


def windows_of(parity, everything):
    return pl.pallas_call(
        window_kernel,
        out_shape=jax.ShapeDtypeStruct((16, 112, 128), BF16),
        in_specs=[pl.BlockSpec(memory_space=pltpu.SMEM), pl.BlockSpec(memory_space=pltpu.VMEM)],
        out_specs=pl.BlockSpec(memory_space=pltpu.VMEM),
        cost_estimate=pl.CostEstimate(flops=0, bytes_accessed=700_000, transcendentals=0),
        compiler_params=pltpu.CompilerParams(vmem_limit_bytes=16 * 2**20),
        name="windows",
    )(parity, everything)


def attend(block, queries, window):
    return pl.pallas_call(
        attend_kernel,
        out_shape=jax.ShapeDtypeStruct((BLOCK, 2 * HD), BF16),
        in_specs=[
            pl.BlockSpec(memory_space=pltpu.SMEM),
            pl.BlockSpec(memory_space=pltpu.VMEM),
            pl.BlockSpec(memory_space=pltpu.VMEM),
        ],
        out_specs=pl.BlockSpec(memory_space=pltpu.VMEM),
        scratch_shapes=[
            pltpu.VMEM((HD, 5 * BLOCK), BF16),
            pltpu.VMEM((5 * BLOCK, 2 * HD), BF16),
            pltpu.VMEM((W2 + BLOCK, HD), F32),
            pltpu.VMEM((W2 + BLOCK, HD), F32),
            pltpu.VMEM((W2 + BLOCK, HD), F32),
            pltpu.VMEM((BLOCK, 2 * HD), F32),
            pltpu.VMEM((BLOCK, 2 * HD), F32),
        ],
        cost_estimate=pl.CostEstimate(flops=6_000_000_000, bytes_accessed=1_000_000, transcendentals=4_200_000),
        compiler_params=pltpu.CompilerParams(vmem_limit_bytes=16 * 2**20),
        name="attend",
    )(block, queries, window)


def project_kernel(place_ref, a_ref, w0_ref, w1_ref, w2_ref, w3_ref, keep_ref, send_ref):
    core, yl, x = place_ref[0], place_ref[1], place_ref[2]
    for half in range(2):
        for slot in range(2):
            block = lax.bitwise_xor(2 * half + (core if slot == 0 else 1 - core), yl)
            total = jnp.zeros((256, 256), F32)
            for away, w_ref in enumerate((w0_ref, w1_ref, w2_ref, w3_ref)):
                total += jnp.dot(a_ref[lax.bitwise_xor(x, away)], w_ref[block], preferred_element_type=F32)
            if slot == 0:
                keep_ref[half] = total
            else:
                send_ref[half] = total


def project(place, attention, weights):
    return pl.pallas_call(
        project_kernel,
        out_shape=(jax.ShapeDtypeStruct((2, 256, 256), F32), jax.ShapeDtypeStruct((2, 256, 256), F32)),
        in_specs=[pl.BlockSpec(memory_space=pltpu.SMEM)] + [pl.BlockSpec(memory_space=pltpu.VMEM)] * 5,
        out_specs=(pl.BlockSpec(memory_space=pltpu.VMEM), pl.BlockSpec(memory_space=pltpu.VMEM)),
        cost_estimate=pl.CostEstimate(flops=540_000_000, bytes_accessed=4_000_000, transcendentals=0),
        compiler_params=pltpu.CompilerParams(vmem_limit_bytes=16 * 2**20),
        name="project",
    )(place, attention, *weights)


def across(x, axis, away):
    count = lax.axis_size(axis)
    return lax.ppermute(x, axis, [(i, i ^ away) for i in range(count)])


def layer(queries, kv, w_out):
    yh, z, core, yl, x = (lax.axis_index(name).astype(jnp.int32) for name in ALL)
    parity = z % 2
    block = 2 * (4 * yl + x) + parity
    moved = lax.ppermute(w_out, ALL, weight_pairs())
    queries = lax.ppermute(queries, ALL, attention_pairs())
    raw = jnp.transpose(kv, (0, 2, 1))
    other = across(raw, "core", 1)
    pair = jnp.where(core == 0, jnp.stack([raw, other]), jnp.stack([other, raw]))
    everything = lax.all_to_all(jnp.broadcast_to(pair[None], (16,) + pair.shape), ("yh", "z"), 0, 0)
    columns = [moved]
    for away in (1, 2, 3):
        columns.append(across(moved, "yl", away))
    columns = jnp.stack(columns)
    weights = [columns]
    for away in (1, 2, 3):
        weights.append(across(columns, "x", away))
    window = windows_of(parity.reshape(1), everything.reshape(32, 4, 8, 128))
    window = lax.all_to_all(window, HEAD, 0, 0)
    attention = attend(block.reshape(1), queries, window)
    attention = lax.all_to_all(jnp.broadcast_to(attention[None], (8,) + attention.shape), "z", 0, 0)
    keep, send = project(jnp.stack([core, yl, x]), attention.reshape(4, 256, 256), weights)
    got = across(send, "core", 1)
    summed = keep + got
    leaving = lax.dynamic_index_in_dim(summed, 1 - yh, 0, keepdims=False).astype(BF16)
    arrived = across(leaving, "yh", 1)
    staying = lax.dynamic_index_in_dim(summed, yh, 0, keepdims=False)
    return (staying + arrived.astype(F32)).astype(BF16)


def solution(mesh):
    fine = Mesh(mesh.devices.reshape(SIZES), ALL)
    return jax.shard_map(
        layer,
        mesh=fine,
        in_specs=(P(TOK, HEAD), P(None, TOK, HEAD), P(HEAD, TOK)),
        out_specs=P(HEAD, TOK),
        check_vma=False,
    )
```

```python
import math

import jax
import jax.numpy as jnp
from jax import lax
from jax.experimental import pallas as pl
from jax.experimental.pallas import tpu as pltpu
from jax.sharding import Mesh, PartitionSpec as P


HD = 128
W2 = 32
BLOCK = 128
STEP = 8
TOK = ("yh", "z", "core")
HEAD = ("yl", "x")
ALL = TOK + HEAD
SIZES = (2, 8, 2, 4, 4)
FAR = -1e30
BF16 = jnp.bfloat16
F32 = jnp.float32


def flat(yh, z, core, yl, x):
    return (((yh * 8 + z) * 2 + core) * 4 + yl) * 4 + x


def places():
    for yh in range(2):
        for z in range(8):
            for core in range(2):
                for yl in range(4):
                    for x in range(4):
                        yield yh, z, core, yl, x


def attention_pairs():
    return [
        (flat(yh, z, core, yl, x), flat(yl // 2, 2 * x + core, yl % 2, 2 * yh + z // 4, z % 4))
        for yh, z, core, yl, x in places()
    ]


def weight_pairs():
    return [
        (flat(yh, z, core, yl, x), flat(yl // 2, z, yl % 2, 2 * yh + core, x))
        for yh, z, core, yl, x in places()
    ]


def attend_kernel(
    where_ref, q_ref, kv_ref, out_ref, k1_ref, v1_ref, k2_ref, v2_ref, live_ref, q32_ref, acc_ref, even_ref, odd_ref, tops_ref
):
    block = where_ref[0]
    scale = 3.0 / math.sqrt(HD) * math.log2(math.e)
    steps = BLOCK // STEP

    def piece(k):
        return kv_ref[:, 8 * k : 8 * k + 8, :].astype(F32).reshape(HD, BLOCK)

    for k in range(5):
        k1_ref[:, BLOCK * k : BLOCK * (k + 1)] = piece(k).astype(BF16)
        v1_ref[BLOCK * k : BLOCK * (k + 1), 0:HD] = piece(5 + k).T.astype(BF16)
    v1_ref[:, HD : 2 * HD] = jnp.ones((5 * BLOCK, HD), BF16)
    first = block == 0
    own_k2 = piece(11).T
    k2_ref[W2:, :] = own_k2
    k2_ref[0:W2, :] = jnp.where(first, jnp.broadcast_to(own_k2[0:1, :], (W2, HD)), piece(10).T[BLOCK - W2 :, :])
    v2_ref[W2:, :] = piece(13).T
    v2_ref[0:W2, :] = jnp.where(first, 0.0, piece(12).T[BLOCK - W2 :, :])
    live_ref[W2:, :] = jnp.ones((BLOCK, HD), F32)
    live_ref[0:W2, :] = jnp.where(first, jnp.zeros((W2, HD), F32), 1.0)
    q32_ref[...] = q_ref[...].astype(F32)
    bias = [jnp.where(block - 4 + k < 0, FAR, 0.0) for k in range(4)]
    column = lax.broadcasted_iota(jnp.int32, (STEP, BLOCK), 1)
    row = lax.broadcasted_iota(jnp.int32, (STEP, BLOCK), 0)

    def newer_of(start):
        newer = column > row + start
        return newer, jnp.broadcast_to(newer[None], (W2, STEP, BLOCK)).reshape(W2 * STEP, BLOCK)

    def produce(index, head, held_ref, top_ref):
        start = pl.multiple_of(index * STEP, STEP)
        _, newer_all = newer_of(start)
        query = q32_ref[pl.ds(start, STEP), HD * head : HD * (head + 1)]
        rows = [query * k2_ref[pl.ds(start + W2 - back, STEP), :] for back in range(W2)]
        query_key = jnp.concatenate(rows, axis=0).astype(BF16)
        scores = jnp.dot(query_key, k1_ref[...], preferred_element_type=F32)
        held_ref[:, 0:BLOCK] = jnp.where(newer_all, scores[:, 0:BLOCK], scores[:, 4 * BLOCK :])
        held_ref[:, BLOCK:] = scores[:, BLOCK : 4 * BLOCK]
        newer, _ = newer_of(start)
        tile_bias = [jnp.where(newer, bias[0], 0.0)] + [jnp.full((STEP, BLOCK), bias[k], F32) for k in (1, 2, 3)]
        tiles = [jnp.where(newer_all, scores[:, 0:BLOCK], scores[:, 4 * BLOCK :])]
        tiles += [scores[:, BLOCK * k : BLOCK * (k + 1)] for k in (1, 2, 3)]
        peak = None
        for k in range(4):
            top = jnp.max(tiles[k].reshape(W2, STEP, BLOCK), axis=0) + tile_bias[k]
            peak = top if peak is None else jnp.maximum(peak, top)
        top_ref[...] = jnp.broadcast_to(jnp.max(peak, axis=1, keepdims=True) * scale, (STEP, BLOCK))

    def consume(index, head, held_ref, top_ref):
        start = pl.multiple_of(index * STEP, STEP)
        newer, newer_all = newer_of(start)
        tile_bias = [jnp.where(newer, bias[0], 0.0)] + [jnp.full((STEP, BLOCK), bias[k], F32) for k in (1, 2, 3)]
        peak = top_ref[...]
        weights = []
        for k in range(4):
            tile = held_ref[:, BLOCK * k : BLOCK * (k + 1)].reshape(W2, STEP, BLOCK)
            grown = tile * scale + (tile_bias[k] - peak)[None]
            weights.append(jnp.exp2(grown).reshape(W2 * STEP, BLOCK))
        mixed = [jnp.where(newer_all, weights[0], 0.0)] + weights[1:] + [jnp.where(newer_all, 0.0, weights[0])]
        mixed = jnp.concatenate([m.astype(BF16) for m in mixed], axis=1)
        value = jnp.dot(mixed, v1_ref[...], preferred_element_type=F32)
        total = jnp.zeros((STEP, HD), F32)
        denominator = jnp.zeros((STEP, HD), F32)
        for back in range(W2):
            part = value[STEP * back : STEP * (back + 1), :]
            total += part[:, 0:HD] * v2_ref[pl.ds(start + W2 - back, STEP), :]
            denominator += part[:, HD:] * live_ref[pl.ds(start + W2 - back, STEP), :]
        acc_ref[pl.ds(start, STEP), HD * head : HD * (head + 1)] = total / denominator

    for head in range(2):
        produce(0, head, even_ref.at[head], tops_ref.at[head])

    def step(index, carry):
        for head in range(2):
            produce(2 * index + 1, head, odd_ref.at[head], tops_ref.at[2 + head])
            consume(2 * index, head, even_ref.at[head], tops_ref.at[head])
        for head in range(2):
            produce(jnp.minimum(2 * index + 2, steps - 1), head, even_ref.at[head], tops_ref.at[head])
            consume(2 * index + 1, head, odd_ref.at[head], tops_ref.at[2 + head])
        return carry

    lax.fori_loop(0, steps // 2, step, 0)
    out_ref[...] = acc_ref[...].astype(BF16)


def window_kernel(parity_ref, all_ref, out_ref):
    parity = parity_ref[0]
    for column in range(16):
        last = 2 * column + parity
        for k in range(5):
            source = jnp.maximum(last - 4 + k, 0)
            out_ref[column, 8 * k : 8 * (k + 1), :] = all_ref[source, 0]
            out_ref[column, 8 * (5 + k) : 8 * (6 + k), :] = all_ref[source, 1]
        for k in range(2):
            source = jnp.maximum(last - 1 + k, 0)
            out_ref[column, 8 * (10 + k) : 8 * (11 + k), :] = all_ref[source, 2]
            out_ref[column, 8 * (12 + k) : 8 * (13 + k), :] = all_ref[source, 3]


def windows_of(parity, everything):
    return pl.pallas_call(
        window_kernel,
        out_shape=jax.ShapeDtypeStruct((16, 112, 128), BF16),
        in_specs=[pl.BlockSpec(memory_space=pltpu.SMEM), pl.BlockSpec(memory_space=pltpu.VMEM)],
        out_specs=pl.BlockSpec(memory_space=pltpu.VMEM),
        cost_estimate=pl.CostEstimate(flops=0, bytes_accessed=700_000, transcendentals=0),
        compiler_params=pltpu.CompilerParams(vmem_limit_bytes=16 * 2**20),
        name="windows",
    )(parity, everything)


def attend(block, queries, window):
    return pl.pallas_call(
        attend_kernel,
        out_shape=jax.ShapeDtypeStruct((BLOCK, 2 * HD), BF16),
        in_specs=[
            pl.BlockSpec(memory_space=pltpu.SMEM),
            pl.BlockSpec(memory_space=pltpu.VMEM),
            pl.BlockSpec(memory_space=pltpu.VMEM),
        ],
        out_specs=pl.BlockSpec(memory_space=pltpu.VMEM),
        scratch_shapes=[
            pltpu.VMEM((HD, 5 * BLOCK), BF16),
            pltpu.VMEM((5 * BLOCK, 2 * HD), BF16),
            pltpu.VMEM((W2 + BLOCK, HD), F32),
            pltpu.VMEM((W2 + BLOCK, HD), F32),
            pltpu.VMEM((W2 + BLOCK, HD), F32),
            pltpu.VMEM((BLOCK, 2 * HD), F32),
            pltpu.VMEM((BLOCK, 2 * HD), F32),
            pltpu.VMEM((2, W2 * STEP, 4 * BLOCK), F32),
            pltpu.VMEM((2, W2 * STEP, 4 * BLOCK), F32),
            pltpu.VMEM((4, STEP, BLOCK), F32),
        ],
        cost_estimate=pl.CostEstimate(flops=6_000_000_000, bytes_accessed=1_000_000, transcendentals=4_200_000),
        compiler_params=pltpu.CompilerParams(vmem_limit_bytes=16 * 2**20),
        name="attend",
    )(block, queries, window)


def project_kernel(place_ref, a_ref, w0_ref, w1_ref, w2_ref, w3_ref, keep_ref, send_ref):
    core, yl, x = place_ref[0], place_ref[1], place_ref[2]
    for half in range(2):
        for slot in range(2):
            block = lax.bitwise_xor(2 * half + (core if slot == 0 else 1 - core), yl)
            total = jnp.zeros((256, 256), F32)
            for away, w_ref in enumerate((w0_ref, w1_ref, w2_ref, w3_ref)):
                total += jnp.dot(a_ref[lax.bitwise_xor(x, away)], w_ref[block], preferred_element_type=F32)
            if slot == 0:
                keep_ref[half] = total
            else:
                send_ref[half] = total


def project(place, attention, weights):
    return pl.pallas_call(
        project_kernel,
        out_shape=(jax.ShapeDtypeStruct((2, 256, 256), F32), jax.ShapeDtypeStruct((2, 256, 256), F32)),
        in_specs=[pl.BlockSpec(memory_space=pltpu.SMEM)] + [pl.BlockSpec(memory_space=pltpu.VMEM)] * 5,
        out_specs=(pl.BlockSpec(memory_space=pltpu.VMEM), pl.BlockSpec(memory_space=pltpu.VMEM)),
        cost_estimate=pl.CostEstimate(flops=540_000_000, bytes_accessed=4_000_000, transcendentals=0),
        compiler_params=pltpu.CompilerParams(vmem_limit_bytes=16 * 2**20),
        name="project",
    )(place, attention, *weights)


def across(x, axis, away):
    count = lax.axis_size(axis)
    return lax.ppermute(x, axis, [(i, i ^ away) for i in range(count)])


def layer(queries, kv, w_out):
    yh, z, core, yl, x = (lax.axis_index(name).astype(jnp.int32) for name in ALL)
    parity = z % 2
    block = 2 * (4 * yl + x) + parity
    moved = lax.ppermute(w_out, ALL, weight_pairs())
    queries = lax.ppermute(queries, ALL, attention_pairs())
    raw = jnp.transpose(kv, (0, 2, 1))
    other = across(raw, "core", 1)
    pair = jnp.where(core == 0, jnp.stack([raw, other]), jnp.stack([other, raw]))
    everything = lax.all_to_all(jnp.broadcast_to(pair[None], (16,) + pair.shape), ("yh", "z"), 0, 0)
    columns = jnp.stack([moved, across(moved, "yl", 1)])
    columns = jnp.concatenate([columns, across(columns, "yl", 2)])
    weights = [columns]
    for away in (1, 2, 3):
        weights.append(across(columns, "x", away))
    window = windows_of(parity.reshape(1), everything.reshape(32, 4, 8, 128))
    window = lax.all_to_all(window, HEAD, 0, 0)
    attention = attend(block.reshape(1), queries, window)
    attention = lax.all_to_all(jnp.broadcast_to(attention[None], (8,) + attention.shape), "z", 0, 0)
    keep, send = project(jnp.stack([core, yl, x]), attention.reshape(4, 256, 256), weights)
    got = across(send, "core", 1)
    summed = keep + got
    leaving = lax.dynamic_index_in_dim(summed, 1 - yh, 0, keepdims=False).astype(BF16)
    arrived = across(leaving, "yh", 1)
    staying = lax.dynamic_index_in_dim(summed, yh, 0, keepdims=False)
    return (staying + arrived.astype(F32)).astype(BF16)


def solution(mesh):
    fine = Mesh(mesh.devices.reshape(SIZES), ALL)
    return jax.shard_map(
        layer,
        mesh=fine,
        in_specs=(P(TOK, HEAD), P(None, TOK, HEAD), P(HEAD, TOK)),
        out_specs=P(HEAD, TOK),
        check_vma=False,
    )
```

```python
import math

import jax
import jax.numpy as jnp
from jax import lax
from jax.experimental import pallas as pl
from jax.experimental.pallas import tpu as pltpu
from jax.sharding import Mesh, PartitionSpec as P


HD = 128
W2 = 32
BLOCK = 128
STEP = 8
TOK = ("yh", "z", "core")
HEAD = ("yl", "x")
ALL = TOK + HEAD
SIZES = (2, 8, 2, 4, 4)
FAR = -1e30
BF16 = jnp.bfloat16
F32 = jnp.float32


def flat(yh, z, core, yl, x):
    return (((yh * 8 + z) * 2 + core) * 4 + yl) * 4 + x


def places():
    for yh in range(2):
        for z in range(8):
            for core in range(2):
                for yl in range(4):
                    for x in range(4):
                        yield yh, z, core, yl, x


def attention_pairs():
    return [
        (flat(yh, z, core, yl, x), flat(yl // 2, 2 * x + core, yl % 2, 2 * yh + z // 4, z % 4))
        for yh, z, core, yl, x in places()
    ]


def weight_pairs():
    return [
        (flat(yh, z, core, yl, x), flat(yl // 2, z, yl % 2, 2 * yh + core, x))
        for yh, z, core, yl, x in places()
    ]


def attend_kernel(
    where_ref, q_ref, kv_ref, out_ref, k1_ref, v1_ref, k2_ref, v2_ref, live_ref, q32_ref, acc_ref, even_ref, odd_ref, tops_ref
):
    block = where_ref[0]
    scale = 3.0 / math.sqrt(HD) * math.log2(math.e)
    steps = BLOCK // STEP

    def piece(k):
        return kv_ref[:, 8 * k : 8 * k + 8, :].astype(F32).reshape(HD, BLOCK)

    for k in range(5):
        k1_ref[:, BLOCK * k : BLOCK * (k + 1)] = piece(k).astype(BF16)
        v1_ref[BLOCK * k : BLOCK * (k + 1), 0:HD] = piece(5 + k).T.astype(BF16)
    v1_ref[:, HD : 2 * HD] = jnp.ones((5 * BLOCK, HD), BF16)
    first = block == 0
    own_k2 = piece(11).T
    k2_ref[W2:, :] = own_k2
    k2_ref[0:W2, :] = jnp.where(first, jnp.broadcast_to(own_k2[0:1, :], (W2, HD)), piece(10).T[BLOCK - W2 :, :])
    v2_ref[W2:, :] = piece(13).T
    v2_ref[0:W2, :] = jnp.where(first, 0.0, piece(12).T[BLOCK - W2 :, :])
    live_ref[W2:, :] = jnp.ones((BLOCK, HD), F32)
    live_ref[0:W2, :] = jnp.where(first, jnp.zeros((W2, HD), F32), 1.0)
    q32_ref[...] = q_ref[...].astype(F32)
    bias = [jnp.where(block - 4 + k < 0, FAR, 0.0) for k in range(4)]
    column = lax.broadcasted_iota(jnp.int32, (STEP, BLOCK), 1)
    row = lax.broadcasted_iota(jnp.int32, (STEP, BLOCK), 0)

    def newer_of(start):
        newer = column > row + start
        return newer, jnp.broadcast_to(newer[None], (W2, STEP, BLOCK)).reshape(W2 * STEP, BLOCK)

    def produce(index, head, held_ref, top_ref):
        start = pl.multiple_of(index * STEP, STEP)
        _, newer_all = newer_of(start)
        query = q32_ref[pl.ds(start, STEP), HD * head : HD * (head + 1)]
        rows = [query * k2_ref[pl.ds(start + W2 - back, STEP), :] for back in range(W2)]
        query_key = jnp.concatenate(rows, axis=0).astype(BF16)
        scores = jnp.dot(query_key, k1_ref[...], preferred_element_type=F32)
        held_ref[:, 0:BLOCK] = jnp.where(newer_all, scores[:, 0:BLOCK], scores[:, 4 * BLOCK :])
        held_ref[:, BLOCK:] = scores[:, BLOCK : 4 * BLOCK]
        newer, _ = newer_of(start)
        tile_bias = [jnp.where(newer, bias[0], 0.0)] + [jnp.full((STEP, BLOCK), bias[k], F32) for k in (1, 2, 3)]
        tiles = [jnp.where(newer_all, scores[:, 0:BLOCK], scores[:, 4 * BLOCK :])]
        tiles += [scores[:, BLOCK * k : BLOCK * (k + 1)] for k in (1, 2, 3)]
        peak = None
        for k in range(4):
            top = jnp.max(tiles[k].reshape(W2, STEP, BLOCK), axis=0) + tile_bias[k]
            peak = top if peak is None else jnp.maximum(peak, top)
        top_ref[...] = jnp.broadcast_to(jnp.max(peak, axis=1, keepdims=True) * scale, (STEP, BLOCK))

    def consume(index, head, held_ref, top_ref):
        start = pl.multiple_of(index * STEP, STEP)
        newer, newer_all = newer_of(start)
        tile_bias = [jnp.where(newer, bias[0], 0.0)] + [jnp.full((STEP, BLOCK), bias[k], F32) for k in (1, 2, 3)]
        peak = top_ref[...]
        weights = []
        for k in range(4):
            tile = held_ref[:, BLOCK * k : BLOCK * (k + 1)].reshape(W2, STEP, BLOCK)
            grown = tile * scale + (tile_bias[k] - peak)[None]
            weights.append(jnp.exp2(grown).reshape(W2 * STEP, BLOCK))
        mixed = [jnp.where(newer_all, weights[0], 0.0)] + weights[1:] + [jnp.where(newer_all, 0.0, weights[0])]
        mixed = jnp.concatenate([m.astype(BF16) for m in mixed], axis=1)
        value = jnp.dot(mixed, v1_ref[...], preferred_element_type=F32)
        total = jnp.zeros((STEP, HD), F32)
        denominator = jnp.zeros((STEP, HD), F32)
        for back in range(W2):
            part = value[STEP * back : STEP * (back + 1), :]
            total += part[:, 0:HD] * v2_ref[pl.ds(start + W2 - back, STEP), :]
            denominator += part[:, HD:] * live_ref[pl.ds(start + W2 - back, STEP), :]
        acc_ref[pl.ds(start, STEP), HD * head : HD * (head + 1)] = total / denominator

    for head in range(2):
        produce(0, head, even_ref.at[head], tops_ref.at[head])

    def step(index, carry):
        for head in range(2):
            produce(2 * index + 1, head, odd_ref.at[head], tops_ref.at[2 + head])
            consume(2 * index, head, even_ref.at[head], tops_ref.at[head])
        for head in range(2):
            produce(jnp.minimum(2 * index + 2, steps - 1), head, even_ref.at[head], tops_ref.at[head])
            consume(2 * index + 1, head, odd_ref.at[head], tops_ref.at[2 + head])
        return carry

    lax.fori_loop(0, steps // 2, step, 0)
    done = acc_ref[...].astype(BF16)
    for receiver in range(8):
        out_ref[receiver] = done


def window_kernel(parity_ref, all_ref, out_ref):
    parity = parity_ref[0]
    for column in range(16):
        last = 2 * column + parity
        for k in range(5):
            source = jnp.maximum(last - 4 + k, 0)
            out_ref[column, 8 * k : 8 * (k + 1), :] = all_ref[source, 0]
            out_ref[column, 8 * (5 + k) : 8 * (6 + k), :] = all_ref[source, 1]
        for k in range(2):
            source = jnp.maximum(last - 1 + k, 0)
            out_ref[column, 8 * (10 + k) : 8 * (11 + k), :] = all_ref[source, 2]
            out_ref[column, 8 * (12 + k) : 8 * (13 + k), :] = all_ref[source, 3]


def windows_of(parity, everything):
    return pl.pallas_call(
        window_kernel,
        out_shape=jax.ShapeDtypeStruct((16, 112, 128), BF16),
        in_specs=[pl.BlockSpec(memory_space=pltpu.SMEM), pl.BlockSpec(memory_space=pltpu.VMEM)],
        out_specs=pl.BlockSpec(memory_space=pltpu.VMEM),
        cost_estimate=pl.CostEstimate(flops=0, bytes_accessed=700_000, transcendentals=0),
        compiler_params=pltpu.CompilerParams(vmem_limit_bytes=16 * 2**20),
        name="windows",
    )(parity, everything)


def attend(block, queries, window):
    return pl.pallas_call(
        attend_kernel,
        out_shape=jax.ShapeDtypeStruct((8, BLOCK, 2 * HD), BF16),
        in_specs=[
            pl.BlockSpec(memory_space=pltpu.SMEM),
            pl.BlockSpec(memory_space=pltpu.VMEM),
            pl.BlockSpec(memory_space=pltpu.VMEM),
        ],
        out_specs=pl.BlockSpec(memory_space=pltpu.VMEM),
        scratch_shapes=[
            pltpu.VMEM((HD, 5 * BLOCK), BF16),
            pltpu.VMEM((5 * BLOCK, 2 * HD), BF16),
            pltpu.VMEM((W2 + BLOCK, HD), F32),
            pltpu.VMEM((W2 + BLOCK, HD), F32),
            pltpu.VMEM((W2 + BLOCK, HD), F32),
            pltpu.VMEM((BLOCK, 2 * HD), F32),
            pltpu.VMEM((BLOCK, 2 * HD), F32),
            pltpu.VMEM((2, W2 * STEP, 4 * BLOCK), F32),
            pltpu.VMEM((2, W2 * STEP, 4 * BLOCK), F32),
            pltpu.VMEM((4, STEP, BLOCK), F32),
        ],
        cost_estimate=pl.CostEstimate(flops=6_000_000_000, bytes_accessed=1_000_000, transcendentals=4_200_000),
        compiler_params=pltpu.CompilerParams(vmem_limit_bytes=16 * 2**20),
        name="attend",
    )(block, queries, window)


def project_kernel(place_ref, a_ref, w0_ref, w1_ref, w2_ref, w3_ref, keep_ref, send_ref):
    core, yl, x = place_ref[0], place_ref[1], place_ref[2]
    for half in range(2):
        for slot in range(2):
            block = lax.bitwise_xor(2 * half + (core if slot == 0 else 1 - core), yl)
            total = jnp.zeros((256, 256), F32)
            for away, w_ref in enumerate((w0_ref, w1_ref, w2_ref, w3_ref)):
                total += jnp.dot(a_ref[lax.bitwise_xor(x, away)], w_ref[block], preferred_element_type=F32)
            if slot == 0:
                keep_ref[half] = total
            else:
                send_ref[half] = total


def project(place, attention, weights):
    return pl.pallas_call(
        project_kernel,
        out_shape=(jax.ShapeDtypeStruct((2, 256, 256), F32), jax.ShapeDtypeStruct((2, 256, 256), F32)),
        in_specs=[pl.BlockSpec(memory_space=pltpu.SMEM)] + [pl.BlockSpec(memory_space=pltpu.VMEM)] * 5,
        out_specs=(pl.BlockSpec(memory_space=pltpu.VMEM), pl.BlockSpec(memory_space=pltpu.VMEM)),
        cost_estimate=pl.CostEstimate(flops=540_000_000, bytes_accessed=4_000_000, transcendentals=0),
        compiler_params=pltpu.CompilerParams(vmem_limit_bytes=16 * 2**20),
        name="project",
    )(place, attention, *weights)


def across(x, axis, away):
    count = lax.axis_size(axis)
    return lax.ppermute(x, axis, [(i, i ^ away) for i in range(count)])


def layer(queries, kv, w_out):
    yh, z, core, yl, x = (lax.axis_index(name).astype(jnp.int32) for name in ALL)
    parity = z % 2
    block = 2 * (4 * yl + x) + parity
    moved = lax.ppermute(w_out, ALL, weight_pairs())
    queries = lax.ppermute(queries, ALL, attention_pairs())
    raw = jnp.transpose(kv, (0, 2, 1))
    other = across(raw, "core", 1)
    pair = jnp.where(core == 0, jnp.stack([raw, other]), jnp.stack([other, raw]))
    everything = lax.all_to_all(jnp.broadcast_to(pair[None], (16,) + pair.shape), ("yh", "z"), 0, 0)
    columns = [moved]
    for away in (1, 2, 3):
        columns.append(across(moved, "yl", away))
    columns = jnp.stack(columns)
    weights = [columns]
    for away in (1, 2, 3):
        weights.append(across(columns, "x", away))
    window = windows_of(parity.reshape(1), everything.reshape(32, 4, 8, 128))
    window = lax.all_to_all(window, HEAD, 0, 0)
    attention = attend(block.reshape(1), queries, window)
    attention = lax.all_to_all(attention, "z", 0, 0)
    keep, send = project(jnp.stack([core, yl, x]), attention.reshape(4, 256, 256), weights)
    got = across(send, "core", 1)
    summed = keep + got
    leaving = lax.dynamic_index_in_dim(summed, 1 - yh, 0, keepdims=False).astype(BF16)
    arrived = across(leaving, "yh", 1)
    staying = lax.dynamic_index_in_dim(summed, yh, 0, keepdims=False)
    return (staying + arrived.astype(F32)).astype(BF16)


def solution(mesh):
    fine = Mesh(mesh.devices.reshape(SIZES), ALL)
    return jax.shard_map(
        layer,
        mesh=fine,
        in_specs=(P(TOK, HEAD), P(None, TOK, HEAD), P(HEAD, TOK)),
        out_specs=P(HEAD, TOK),
        check_vma=False,
    )
```

```python
import math

import jax
import jax.numpy as jnp
from jax import lax
from jax.experimental import pallas as pl
from jax.experimental.pallas import tpu as pltpu
from jax.sharding import Mesh, PartitionSpec as P


HD = 128
W2 = 32
BLOCK = 128
STEP = 8
TOK = ("yh", "z", "core")
HEAD = ("yl", "x")
ALL = TOK + HEAD
SIZES = (2, 8, 2, 4, 4)
FAR = -1e30
BF16 = jnp.bfloat16
F32 = jnp.float32


def flat(yh, z, core, yl, x):
    return (((yh * 8 + z) * 2 + core) * 4 + yl) * 4 + x


def places():
    for yh in range(2):
        for z in range(8):
            for core in range(2):
                for yl in range(4):
                    for x in range(4):
                        yield yh, z, core, yl, x


def attention_pairs():
    return [
        (flat(yh, z, core, yl, x), flat(yl // 2, 2 * x + core, yl % 2, 2 * yh + z // 4, z % 4))
        for yh, z, core, yl, x in places()
    ]


def weight_pairs(away):
    return [
        (flat(yh, z, core, yl, x), flat(yl // 2, z, yl % 2, (2 * yh + core) ^ away, x))
        for yh, z, core, yl, x in places()
    ]


def attend_kernel(
    where_ref, q_ref, kv_ref, out_ref, k1_ref, v1_ref, k2_ref, v2_ref, live_ref, q32_ref, acc_ref, even_ref, odd_ref, tops_ref
):
    block = where_ref[0]
    scale = 3.0 / math.sqrt(HD) * math.log2(math.e)
    steps = BLOCK // STEP

    def piece(k):
        return kv_ref[:, 8 * k : 8 * k + 8, :].astype(F32).reshape(HD, BLOCK)

    for k in range(5):
        k1_ref[:, BLOCK * k : BLOCK * (k + 1)] = piece(k).astype(BF16)
        v1_ref[BLOCK * k : BLOCK * (k + 1), 0:HD] = piece(5 + k).T.astype(BF16)
    v1_ref[:, HD : 2 * HD] = jnp.ones((5 * BLOCK, HD), BF16)
    first = block == 0
    own_k2 = piece(11).T
    k2_ref[W2:, :] = own_k2
    k2_ref[0:W2, :] = jnp.where(first, jnp.broadcast_to(own_k2[0:1, :], (W2, HD)), piece(10).T[BLOCK - W2 :, :])
    v2_ref[W2:, :] = piece(13).T
    v2_ref[0:W2, :] = jnp.where(first, 0.0, piece(12).T[BLOCK - W2 :, :])
    live_ref[W2:, :] = jnp.ones((BLOCK, HD), F32)
    live_ref[0:W2, :] = jnp.where(first, jnp.zeros((W2, HD), F32), 1.0)
    q32_ref[...] = q_ref[...].astype(F32)
    bias = [jnp.where(block - 4 + k < 0, FAR, 0.0) for k in range(4)]
    column = lax.broadcasted_iota(jnp.int32, (STEP, BLOCK), 1)
    row = lax.broadcasted_iota(jnp.int32, (STEP, BLOCK), 0)

    def newer_of(start):
        newer = column > row + start
        return newer, jnp.broadcast_to(newer[None], (W2, STEP, BLOCK)).reshape(W2 * STEP, BLOCK)

    def produce(index, head, held_ref, top_ref):
        start = pl.multiple_of(index * STEP, STEP)
        _, newer_all = newer_of(start)
        query = q32_ref[pl.ds(start, STEP), HD * head : HD * (head + 1)]
        rows = [query * k2_ref[pl.ds(start + W2 - back, STEP), :] for back in range(W2)]
        query_key = jnp.concatenate(rows, axis=0).astype(BF16)
        scores = jnp.dot(query_key, k1_ref[...], preferred_element_type=F32)
        held_ref[:, 0:BLOCK] = jnp.where(newer_all, scores[:, 0:BLOCK], scores[:, 4 * BLOCK :])
        held_ref[:, BLOCK:] = scores[:, BLOCK : 4 * BLOCK]
        newer, _ = newer_of(start)
        tile_bias = [jnp.where(newer, bias[0], 0.0)] + [jnp.full((STEP, BLOCK), bias[k], F32) for k in (1, 2, 3)]
        tiles = [jnp.where(newer_all, scores[:, 0:BLOCK], scores[:, 4 * BLOCK :])]
        tiles += [scores[:, BLOCK * k : BLOCK * (k + 1)] for k in (1, 2, 3)]
        peak = None
        for k in range(4):
            top = jnp.max(tiles[k].reshape(W2, STEP, BLOCK), axis=0) + tile_bias[k]
            peak = top if peak is None else jnp.maximum(peak, top)
        top_ref[...] = jnp.broadcast_to(jnp.max(peak, axis=1, keepdims=True) * scale, (STEP, BLOCK))

    def consume(index, head, held_ref, top_ref):
        start = pl.multiple_of(index * STEP, STEP)
        newer, newer_all = newer_of(start)
        tile_bias = [jnp.where(newer, bias[0], 0.0)] + [jnp.full((STEP, BLOCK), bias[k], F32) for k in (1, 2, 3)]
        peak = top_ref[...]
        weights = []
        for k in range(4):
            tile = held_ref[:, BLOCK * k : BLOCK * (k + 1)].reshape(W2, STEP, BLOCK)
            grown = tile * scale + (tile_bias[k] - peak)[None]
            weights.append(jnp.exp2(grown).reshape(W2 * STEP, BLOCK))
        mixed = [jnp.where(newer_all, weights[0], 0.0)] + weights[1:] + [jnp.where(newer_all, 0.0, weights[0])]
        mixed = jnp.concatenate([m.astype(BF16) for m in mixed], axis=1)
        value = jnp.dot(mixed, v1_ref[...], preferred_element_type=F32)
        total = jnp.zeros((STEP, HD), F32)
        denominator = jnp.zeros((STEP, HD), F32)
        for back in range(W2):
            part = value[STEP * back : STEP * (back + 1), :]
            total += part[:, 0:HD] * v2_ref[pl.ds(start + W2 - back, STEP), :]
            denominator += part[:, HD:] * live_ref[pl.ds(start + W2 - back, STEP), :]
        acc_ref[pl.ds(start, STEP), HD * head : HD * (head + 1)] = total / denominator

    for head in range(2):
        produce(0, head, even_ref.at[head], tops_ref.at[head])

    def step(index, carry):
        for head in range(2):
            produce(2 * index + 1, head, odd_ref.at[head], tops_ref.at[2 + head])
            consume(2 * index, head, even_ref.at[head], tops_ref.at[head])
        for head in range(2):
            produce(jnp.minimum(2 * index + 2, steps - 1), head, even_ref.at[head], tops_ref.at[head])
            consume(2 * index + 1, head, odd_ref.at[head], tops_ref.at[2 + head])
        return carry

    lax.fori_loop(0, steps // 2, step, 0)
    done = acc_ref[...].astype(BF16)
    for receiver in range(8):
        out_ref[receiver] = done


def window_kernel(parity_ref, all_ref, out_ref):
    parity = parity_ref[0]
    for column in range(16):
        last = 2 * column + parity
        for k in range(5):
            source = jnp.maximum(last - 4 + k, 0)
            out_ref[column, 8 * k : 8 * (k + 1), :] = all_ref[source, 0]
            out_ref[column, 8 * (5 + k) : 8 * (6 + k), :] = all_ref[source, 1]
        for k in range(2):
            source = jnp.maximum(last - 1 + k, 0)
            out_ref[column, 8 * (10 + k) : 8 * (11 + k), :] = all_ref[source, 2]
            out_ref[column, 8 * (12 + k) : 8 * (13 + k), :] = all_ref[source, 3]


def windows_of(parity, everything):
    return pl.pallas_call(
        window_kernel,
        out_shape=jax.ShapeDtypeStruct((16, 112, 128), BF16),
        in_specs=[pl.BlockSpec(memory_space=pltpu.SMEM), pl.BlockSpec(memory_space=pltpu.VMEM)],
        out_specs=pl.BlockSpec(memory_space=pltpu.VMEM),
        cost_estimate=pl.CostEstimate(flops=0, bytes_accessed=700_000, transcendentals=0),
        compiler_params=pltpu.CompilerParams(vmem_limit_bytes=16 * 2**20),
        name="windows",
    )(parity, everything)


def attend(block, queries, window):
    return pl.pallas_call(
        attend_kernel,
        out_shape=jax.ShapeDtypeStruct((8, BLOCK, 2 * HD), BF16),
        in_specs=[
            pl.BlockSpec(memory_space=pltpu.SMEM),
            pl.BlockSpec(memory_space=pltpu.VMEM),
            pl.BlockSpec(memory_space=pltpu.VMEM),
        ],
        out_specs=pl.BlockSpec(memory_space=pltpu.VMEM),
        scratch_shapes=[
            pltpu.VMEM((HD, 5 * BLOCK), BF16),
            pltpu.VMEM((5 * BLOCK, 2 * HD), BF16),
            pltpu.VMEM((W2 + BLOCK, HD), F32),
            pltpu.VMEM((W2 + BLOCK, HD), F32),
            pltpu.VMEM((W2 + BLOCK, HD), F32),
            pltpu.VMEM((BLOCK, 2 * HD), F32),
            pltpu.VMEM((BLOCK, 2 * HD), F32),
            pltpu.VMEM((2, W2 * STEP, 4 * BLOCK), F32),
            pltpu.VMEM((2, W2 * STEP, 4 * BLOCK), F32),
            pltpu.VMEM((4, STEP, BLOCK), F32),
        ],
        cost_estimate=pl.CostEstimate(flops=6_000_000_000, bytes_accessed=1_000_000, transcendentals=4_200_000),
        compiler_params=pltpu.CompilerParams(vmem_limit_bytes=16 * 2**20),
        name="attend",
    )(block, queries, window)


def project_kernel(place_ref, a_ref, w0_ref, w1_ref, w2_ref, w3_ref, keep_ref, send_ref):
    core, yl, x = place_ref[0], place_ref[1], place_ref[2]
    for half in range(2):
        for slot in range(2):
            block = lax.bitwise_xor(2 * half + (core if slot == 0 else 1 - core), yl)
            total = jnp.zeros((256, 256), F32)
            for away, w_ref in enumerate((w0_ref, w1_ref, w2_ref, w3_ref)):
                total += jnp.dot(a_ref[lax.bitwise_xor(x, away)], w_ref[block], preferred_element_type=F32)
            if slot == 0:
                keep_ref[half] = total
            else:
                send_ref[half] = total


def project(place, attention, weights):
    return pl.pallas_call(
        project_kernel,
        out_shape=(jax.ShapeDtypeStruct((2, 256, 256), F32), jax.ShapeDtypeStruct((2, 256, 256), F32)),
        in_specs=[pl.BlockSpec(memory_space=pltpu.SMEM)] + [pl.BlockSpec(memory_space=pltpu.VMEM)] * 5,
        out_specs=(pl.BlockSpec(memory_space=pltpu.VMEM), pl.BlockSpec(memory_space=pltpu.VMEM)),
        cost_estimate=pl.CostEstimate(flops=540_000_000, bytes_accessed=4_000_000, transcendentals=0),
        compiler_params=pltpu.CompilerParams(vmem_limit_bytes=16 * 2**20),
        name="project",
    )(place, attention, *weights)


def across(x, axis, away):
    count = lax.axis_size(axis)
    return lax.ppermute(x, axis, [(i, i ^ away) for i in range(count)])


def layer(queries, kv, w_out):
    yh, z, core, yl, x = (lax.axis_index(name).astype(jnp.int32) for name in ALL)
    parity = z % 2
    block = 2 * (4 * yl + x) + parity
    moved = lax.ppermute(w_out, ALL, weight_pairs(0))
    queries = lax.ppermute(queries, ALL, attention_pairs())
    raw = jnp.transpose(kv, (0, 2, 1))
    other = across(raw, "core", 1)
    pair = jnp.where(core == 0, jnp.stack([raw, other]), jnp.stack([other, raw]))
    everything = lax.all_to_all(jnp.broadcast_to(pair[None], (16,) + pair.shape), ("yh", "z"), 0, 0)
    columns = jnp.stack([moved, lax.ppermute(w_out, ALL, weight_pairs(2))])
    across_row = across(columns, "yl", 1)
    columns = jnp.stack([columns[0], across_row[0], columns[1], across_row[1]])
    weights = [columns]
    for away in (1, 2, 3):
        weights.append(across(columns, "x", away))
    window = windows_of(parity.reshape(1), everything.reshape(32, 4, 8, 128))
    window = lax.all_to_all(window, HEAD, 0, 0)
    attention = attend(block.reshape(1), queries, window)
    attention = lax.all_to_all(attention, "z", 0, 0)
    keep, send = project(jnp.stack([core, yl, x]), attention.reshape(4, 256, 256), weights)
    got = across(send, "core", 1)
    summed = keep + got
    leaving = lax.dynamic_index_in_dim(summed, 1 - yh, 0, keepdims=False).astype(BF16)
    arrived = across(leaving, "yh", 1)
    staying = lax.dynamic_index_in_dim(summed, yh, 0, keepdims=False)
    return (staying + arrived.astype(F32)).astype(BF16)


def solution(mesh):
    fine = Mesh(mesh.devices.reshape(SIZES), ALL)
    return jax.shard_map(
        layer,
        mesh=fine,
        in_specs=(P(TOK, HEAD), P(None, TOK, HEAD), P(HEAD, TOK)),
        out_specs=P(HEAD, TOK),
        check_vma=False,
    )
```

```python
import math

import jax
import jax.numpy as jnp
from jax import lax
from jax.experimental import pallas as pl
from jax.experimental.pallas import tpu as pltpu
from jax.sharding import Mesh, PartitionSpec as P


HD = 128
W2 = 32
BLOCK = 128
STEP = 8
TOK = ("yh", "z", "core")
HEAD = ("yl", "x")
ALL = TOK + HEAD
SIZES = (2, 8, 2, 4, 4)
FAR = -1e30
BF16 = jnp.bfloat16
F32 = jnp.float32


def flat(yh, z, core, yl, x):
    return (((yh * 8 + z) * 2 + core) * 4 + yl) * 4 + x


def places():
    for yh in range(2):
        for z in range(8):
            for core in range(2):
                for yl in range(4):
                    for x in range(4):
                        yield yh, z, core, yl, x


def attention_pairs():
    return [
        (flat(yh, z, core, yl, x), flat(yl // 2, 2 * x + core, yl % 2, 2 * yh + z // 4, z % 4))
        for yh, z, core, yl, x in places()
    ]


def weight_pairs(away):
    return [
        (flat(yh, z, core, yl, x), flat(yl // 2, z, yl % 2, (2 * yh + core) ^ away, x))
        for yh, z, core, yl, x in places()
    ]


def attend_kernel(
    where_ref, q_ref, kv_ref, out_ref, k1_ref, v1_ref, k2_ref, v2_ref, live_ref, q32_ref, acc_ref, even_ref, odd_ref, tops_ref
):
    block = where_ref[0]
    scale = 3.0 / math.sqrt(HD) * math.log2(math.e)
    steps = BLOCK // STEP

    def piece(k):
        return kv_ref[:, 8 * k : 8 * k + 8, :].astype(F32).reshape(HD, BLOCK)

    for k in range(5):
        k1_ref[:, BLOCK * k : BLOCK * (k + 1)] = piece(k).astype(BF16)
        v1_ref[BLOCK * k : BLOCK * (k + 1), 0:HD] = piece(5 + k).T.astype(BF16)
    v1_ref[:, HD : 2 * HD] = jnp.ones((5 * BLOCK, HD), BF16)
    first = block == 0
    own_k2 = piece(11).T
    k2_ref[W2:, :] = own_k2
    k2_ref[0:W2, :] = jnp.where(first, jnp.broadcast_to(own_k2[0:1, :], (W2, HD)), piece(10).T[BLOCK - W2 :, :])
    v2_ref[W2:, :] = piece(13).T
    v2_ref[0:W2, :] = jnp.where(first, 0.0, piece(12).T[BLOCK - W2 :, :])
    live_ref[W2:, :] = jnp.ones((BLOCK, HD), F32)
    live_ref[0:W2, :] = jnp.where(first, jnp.zeros((W2, HD), F32), 1.0)
    q32_ref[...] = q_ref[...].astype(F32)
    bias = [jnp.where(block - 4 + k < 0, FAR, 0.0) for k in range(4)]
    column = lax.broadcasted_iota(jnp.int32, (STEP, BLOCK), 1)
    row = lax.broadcasted_iota(jnp.int32, (STEP, BLOCK), 0)

    def newer_of(start):
        newer = column > row + start
        return newer, jnp.broadcast_to(newer[None], (W2, STEP, BLOCK)).reshape(W2 * STEP, BLOCK)

    def produce(index, head, held_ref, top_ref):
        start = pl.multiple_of(index * STEP, STEP)
        _, newer_all = newer_of(start)
        query = q32_ref[pl.ds(start, STEP), HD * head : HD * (head + 1)]
        rows = [query * k2_ref[pl.ds(start + W2 - back, STEP), :] for back in range(W2)]
        query_key = jnp.concatenate(rows, axis=0).astype(BF16)
        scores = jnp.dot(query_key, k1_ref[...], preferred_element_type=F32)
        held_ref[:, 0:BLOCK] = jnp.where(newer_all, scores[:, 0:BLOCK], scores[:, 4 * BLOCK :])
        held_ref[:, BLOCK:] = scores[:, BLOCK : 4 * BLOCK]
        newer, _ = newer_of(start)
        tile_bias = [jnp.where(newer, bias[0], 0.0)] + [jnp.full((STEP, BLOCK), bias[k], F32) for k in (1, 2, 3)]
        tiles = [jnp.where(newer_all, scores[:, 0:BLOCK], scores[:, 4 * BLOCK :])]
        tiles += [scores[:, BLOCK * k : BLOCK * (k + 1)] for k in (1, 2, 3)]
        peak = None
        for k in range(4):
            top = jnp.max(tiles[k].reshape(W2, STEP, BLOCK), axis=0) + tile_bias[k]
            peak = top if peak is None else jnp.maximum(peak, top)
        top_ref[...] = jnp.broadcast_to(jnp.max(peak, axis=1, keepdims=True) * scale, (STEP, BLOCK))

    def consume(index, head, held_ref, top_ref):
        start = pl.multiple_of(index * STEP, STEP)
        newer, newer_all = newer_of(start)
        tile_bias = [jnp.where(newer, bias[0], 0.0)] + [jnp.full((STEP, BLOCK), bias[k], F32) for k in (1, 2, 3)]
        peak = top_ref[...]
        weights = []
        for k in range(4):
            tile = held_ref[:, BLOCK * k : BLOCK * (k + 1)].reshape(W2, STEP, BLOCK)
            grown = tile * scale + (tile_bias[k] - peak)[None]
            weights.append(jnp.exp2(grown).reshape(W2 * STEP, BLOCK))
        mixed = [jnp.where(newer_all, weights[0], 0.0)] + weights[1:] + [jnp.where(newer_all, 0.0, weights[0])]
        mixed = jnp.concatenate([m.astype(BF16) for m in mixed], axis=1)
        value = jnp.dot(mixed, v1_ref[...], preferred_element_type=F32)
        total = jnp.zeros((STEP, HD), F32)
        denominator = jnp.zeros((STEP, HD), F32)
        for back in range(W2):
            part = value[STEP * back : STEP * (back + 1), :]
            total += part[:, 0:HD] * v2_ref[pl.ds(start + W2 - back, STEP), :]
            denominator += part[:, HD:] * live_ref[pl.ds(start + W2 - back, STEP), :]
        acc_ref[pl.ds(start, STEP), HD * head : HD * (head + 1)] = total / denominator

    for head in range(2):
        produce(0, head, even_ref.at[head], tops_ref.at[head])

    def step(index, carry):
        for head in range(2):
            produce(2 * index + 1, head, odd_ref.at[head], tops_ref.at[2 + head])
            consume(2 * index, head, even_ref.at[head], tops_ref.at[head])
        for head in range(2):
            produce(jnp.minimum(2 * index + 2, steps - 1), head, even_ref.at[head], tops_ref.at[head])
            consume(2 * index + 1, head, odd_ref.at[head], tops_ref.at[2 + head])
        return carry

    lax.fori_loop(0, steps // 2, step, 0)
    done = acc_ref[...].astype(BF16)
    for receiver in range(8):
        out_ref[receiver] = done


def window_kernel(parity_ref, all_ref, out_ref):
    parity = parity_ref[0]
    for column in range(16):
        last = 2 * column + parity
        for k in range(5):
            source = jnp.maximum(last - 4 + k, 0)
            out_ref[column, 8 * k : 8 * (k + 1), :] = all_ref[source, 0]
            out_ref[column, 8 * (5 + k) : 8 * (6 + k), :] = all_ref[source, 1]
        for k in range(2):
            source = jnp.maximum(last - 1 + k, 0)
            out_ref[column, 8 * (10 + k) : 8 * (11 + k), :] = all_ref[source, 2]
            out_ref[column, 8 * (12 + k) : 8 * (13 + k), :] = all_ref[source, 3]


def windows_of(parity, everything):
    return pl.pallas_call(
        window_kernel,
        out_shape=jax.ShapeDtypeStruct((16, 112, 128), BF16),
        in_specs=[pl.BlockSpec(memory_space=pltpu.SMEM), pl.BlockSpec(memory_space=pltpu.VMEM)],
        out_specs=pl.BlockSpec(memory_space=pltpu.VMEM),
        cost_estimate=pl.CostEstimate(flops=0, bytes_accessed=700_000, transcendentals=0),
        compiler_params=pltpu.CompilerParams(vmem_limit_bytes=16 * 2**20),
        name="windows",
    )(parity, everything)


def attend(block, queries, window):
    return pl.pallas_call(
        attend_kernel,
        out_shape=jax.ShapeDtypeStruct((8, BLOCK, 2 * HD), BF16),
        in_specs=[
            pl.BlockSpec(memory_space=pltpu.SMEM),
            pl.BlockSpec(memory_space=pltpu.VMEM),
            pl.BlockSpec(memory_space=pltpu.VMEM),
        ],
        out_specs=pl.BlockSpec(memory_space=pltpu.VMEM),
        scratch_shapes=[
            pltpu.VMEM((HD, 5 * BLOCK), BF16),
            pltpu.VMEM((5 * BLOCK, 2 * HD), BF16),
            pltpu.VMEM((W2 + BLOCK, HD), F32),
            pltpu.VMEM((W2 + BLOCK, HD), F32),
            pltpu.VMEM((W2 + BLOCK, HD), F32),
            pltpu.VMEM((BLOCK, 2 * HD), F32),
            pltpu.VMEM((BLOCK, 2 * HD), F32),
            pltpu.VMEM((2, W2 * STEP, 4 * BLOCK), F32),
            pltpu.VMEM((2, W2 * STEP, 4 * BLOCK), F32),
            pltpu.VMEM((4, STEP, BLOCK), F32),
        ],
        cost_estimate=pl.CostEstimate(flops=6_000_000_000, bytes_accessed=1_000_000, transcendentals=4_200_000),
        compiler_params=pltpu.CompilerParams(vmem_limit_bytes=16 * 2**20),
        name="attend",
    )(block, queries, window)


def project_kernel(place_ref, a_ref, w0_ref, w1_ref, w2_ref, w3_ref, keep_ref, send_ref):
    core, yl, x = place_ref[0], place_ref[1], place_ref[2]
    for half in range(2):
        for slot in range(2):
            block = lax.bitwise_xor(2 * half + (core if slot == 0 else 1 - core), yl)
            total = jnp.zeros((256, 256), F32)
            for away, w_ref in enumerate((w0_ref, w1_ref, w2_ref, w3_ref)):
                total += jnp.dot(a_ref[lax.bitwise_xor(x, away)], w_ref[block], preferred_element_type=F32)
            if slot == 0:
                keep_ref[half] = total
            else:
                send_ref[half] = total.astype(BF16)


def project(place, attention, weights):
    return pl.pallas_call(
        project_kernel,
        out_shape=(jax.ShapeDtypeStruct((2, 256, 256), F32), jax.ShapeDtypeStruct((2, 256, 256), BF16)),
        in_specs=[pl.BlockSpec(memory_space=pltpu.SMEM)] + [pl.BlockSpec(memory_space=pltpu.VMEM)] * 5,
        out_specs=(pl.BlockSpec(memory_space=pltpu.VMEM), pl.BlockSpec(memory_space=pltpu.VMEM)),
        cost_estimate=pl.CostEstimate(flops=540_000_000, bytes_accessed=4_000_000, transcendentals=0),
        compiler_params=pltpu.CompilerParams(vmem_limit_bytes=16 * 2**20),
        name="project",
    )(place, attention, *weights)


def across(x, axis, away):
    count = lax.axis_size(axis)
    return lax.ppermute(x, axis, [(i, i ^ away) for i in range(count)])


def layer(queries, kv, w_out):
    yh, z, core, yl, x = (lax.axis_index(name).astype(jnp.int32) for name in ALL)
    parity = z % 2
    block = 2 * (4 * yl + x) + parity
    moved = lax.ppermute(w_out, ALL, weight_pairs(0))
    queries = lax.ppermute(queries, ALL, attention_pairs())
    raw = jnp.transpose(kv, (0, 2, 1))
    other = across(raw, "core", 1)
    pair = jnp.where(core == 0, jnp.stack([raw, other]), jnp.stack([other, raw]))
    everything = lax.all_to_all(jnp.broadcast_to(pair[None], (16,) + pair.shape), ("yh", "z"), 0, 0)
    columns = jnp.stack([moved, lax.ppermute(w_out, ALL, weight_pairs(2))])
    across_row = across(columns, "yl", 1)
    columns = jnp.stack([columns[0], across_row[0], columns[1], across_row[1]])
    weights = [columns]
    for away in (1, 2, 3):
        weights.append(across(columns, "x", away))
    window = windows_of(parity.reshape(1), everything.reshape(32, 4, 8, 128))
    window = lax.all_to_all(window, HEAD, 0, 0)
    attention = attend(block.reshape(1), queries, window)
    attention = lax.all_to_all(attention, "z", 0, 0)
    keep, send = project(jnp.stack([core, yl, x]), attention.reshape(4, 256, 256), weights)
    got = across(send, "core", 1)
    summed = keep + got.astype(F32)
    leaving = lax.dynamic_index_in_dim(summed, 1 - yh, 0, keepdims=False).astype(BF16)
    arrived = across(leaving, "yh", 1)
    staying = lax.dynamic_index_in_dim(summed, yh, 0, keepdims=False)
    return (staying + arrived.astype(F32)).astype(BF16)


def solution(mesh):
    fine = Mesh(mesh.devices.reshape(SIZES), ALL)
    return jax.shard_map(
        layer,
        mesh=fine,
        in_specs=(P(TOK, HEAD), P(None, TOK, HEAD), P(HEAD, TOK)),
        out_specs=P(HEAD, TOK),
        check_vma=False,
    )
```
